512 devices in a mesh: blk: 128 (over z_lo, y, x), off: 4 (over z_hi, core).
Axes of the slice: x: 4, y: 4, z: 16 (z_hi: 2, z_lo: 8; z = z_hi * 8 + z_lo), core: 2. Of those that a mesh axis runs over, the one named last changes fastest.
Arguments:
- coefficients: bfloat16 [2048, 32, 128], P('blk', 'off'), may hold values from -12 to 12
Outputs:
- smoothed: float32 [2048, 32, 128], P(('blk', 'off'))
- log_degree: float32 [2048], P(('blk', 'off'))
The draws below stay inside these ranges and needn't reach their ends.
All inputs are finite; a program needn't handle non-finite values.
Results may differ from the reference program's by a relative error of at most 0.005.
Values may be sent and summed in bfloat16 or wider, within the bound.
A program may use at most 64 MiB of HBM per device.

```python
import math
import jax
import jax.numpy as jnp
from jax import lax

R = 32
A = 128
BLK = 16
NIMG = 2048
NCLASS = 128
WINDOW = 32


def draw_coefficients(key, part):
    base_key = jax.random.fold_in(key, 7)
    template_key, label_key, angle_key, noise_key = jax.random.split(base_key, 4)
    half_width = A // 2
    noise_level = 1.6
    templates = jax.random.truncated_normal(template_key, -4.0, 4.0, (NCLASS, R, A), jnp.float32)
    labels = jax.random.randint(label_key, (NIMG,), 0, NCLASS)
    angles = jax.random.uniform(angle_key, (NIMG,), jnp.float32, 0.0, 2.0 * math.pi)
    noise = noise_level * jax.random.truncated_normal(noise_key, -4.0, 4.0, (NIMG, R, A), jnp.float32)
    picked = templates[labels]
    frequency = jnp.arange(half_width, dtype=jnp.float32)
    phase = angles[:, None] * frequency[None, :]
    cos_phase = jnp.cos(phase)[:, None, :]
    sin_phase = jnp.sin(phase)[:, None, :]
    real_part = picked[:, :, :half_width]
    imag_part = picked[:, :, half_width:]
    rotated_real = real_part * cos_phase + imag_part * sin_phase
    rotated_imag = imag_part * cos_phase - real_part * sin_phase
    rotated = jnp.concatenate([rotated_real, rotated_imag], axis=2)
    return (rotated + noise).astype(jnp.bfloat16)


def setup_inputs(seed: int = 0) -> dict:
    key_of = jax.random.split(jax.random.key(seed), 2)
    return {
        "coefficients": draw_coefficients(jax.random.fold_in(key_of[1], 71), 0),
    }


epsilon = 1e-06
concentration = 40.0

def angle_tables(angular):
    half_width = angular // 2
    frequency = jnp.arange(half_width, dtype=jnp.int32)
    shifts = jnp.arange(angular, dtype=jnp.int32)
    product = frequency[:, None] * shifts[None, :] % angular
    phase = product.astype(jnp.float32) * (2.0 * math.pi / angular)
    forward = jnp.concatenate([jnp.cos(phase), -jnp.sin(phase)], axis=0)
    return forward

def reference(coefficients):
    half_width = A // 2
    forward = angle_tables(A)
    backward = forward.T
    values = coefficients.astype(jnp.float32)
    inverse_norm = lax.rsqrt(lax.optimization_barrier(jnp.sum(values * values, axis=(1, 2))) + epsilon)
    swapped = jnp.concatenate([values[:, :, half_width:], values[:, :, :half_width]], axis=2)
    block_count = NIMG // BLK
    block_numbers = jnp.arange(block_count, dtype=jnp.int32)
    highest = lax.Precision.HIGHEST

    def one_block(block_number):
        start = (block_number * BLK).astype(jnp.int32)
        own_block = lax.dynamic_slice_in_dim(values, start, BLK, 0)
        own_inverse = lax.dynamic_slice_in_dim(inverse_norm, start, BLK, 0)
        window_blocks = (block_number + jnp.arange(WINDOW, dtype=jnp.int32)) % block_count
        col_ids = (window_blocks[:, None] * BLK + jnp.arange(BLK, dtype=jnp.int32)[None, :]).reshape(-1)
        col_ids = col_ids.astype(jnp.int32)
        partner = jnp.take(values, col_ids, axis=0)
        partner_swapped = jnp.take(swapped, col_ids, axis=0)
        partner_inverse = jnp.take(inverse_norm, col_ids, axis=0)
        direct = jnp.einsum('irc,jrc->ijc', own_block, partner, precision=highest)
        mixed_terms = jnp.einsum('irc,jrc->ijc', own_block, partner_swapped, precision=highest)
        real_part = direct[:, :, :half_width] + direct[:, :, half_width:]
        imag_part = mixed_terms[:, :, half_width:] - mixed_terms[:, :, :half_width]
        cross_spectrum = jnp.concatenate([real_part, imag_part], axis=2)
        correlation = jnp.einsum('ijq,qs->ijs', cross_spectrum, forward, precision=highest)
        cosine = correlation * own_inverse[:, None, None] * partner_inverse[None, :, None]
        row_ids = start + jnp.arange(BLK, dtype=jnp.int32)
        keep_mask = jnp.where(row_ids[:, None] == col_ids[None, :], 0.0, 1.0).astype(jnp.float32)
        weights = jnp.exp(concentration * cosine) * keep_mask[:, :, None]
        spectral = jnp.einsum('ijs,sq->ijq', weights, backward, precision=highest)
        degree = lax.optimization_barrier(jnp.sum(spectral[:, :, 0], axis=1))
        rounded = spectral.astype(jnp.bfloat16).astype(jnp.float32)
        weight_real = jnp.concatenate([rounded[:, :, :half_width], rounded[:, :, :half_width]], axis=2)
        weight_imag = jnp.concatenate([-rounded[:, :, half_width:], rounded[:, :, half_width:]], axis=2)
        filtered = jnp.einsum('ijc,jrc->irc', weight_real, partner, precision=highest)
        filtered = filtered + jnp.einsum('ijc,jrc->irc', weight_imag, partner_swapped, precision=highest)
        return (filtered, degree)
    filtered, degree = lax.map(one_block, block_numbers)
    filtered = filtered.reshape(NIMG, R, A)
    degree = degree.reshape(NIMG)
    smoothed = filtered / degree[:, None, None]
    return (smoothed, jnp.log(degree))
```

```python
import functools
import math

import jax
import jax.numpy as jnp
from jax import lax
from jax.experimental import pallas as pl
from jax.experimental.pallas import tpu as pltpu
from jax.sharding import PartitionSpec as P

MESH = pl.DeviceIdType.MESH
epsilon = 1e-06
concentration = 40.0
f32, bf16 = jnp.float32, jnp.bfloat16


def nt(a, b):
    return lax.dot_general(a, b, (((1,), (1,)), ((), ())), preferred_element_type=f32)


def nn(a, b):
    return jnp.dot(a, b, preferred_element_type=f32)


def split(a):
    high = a.astype(bf16)
    return high, (a - high.astype(f32)).astype(bf16)


def iota(shape, dim):
    return lax.broadcasted_iota(jnp.int32, shape, dim)


def lane_bit(shape, bit):
    return iota(shape, len(shape) - 1) // bit % 2 == 1


def lane_roll(a, by):
    return pltpu.roll(a, by % 128, a.ndim - 1)


def rotate_parts(a, sign):
    imag = lane_bit(a.shape, 8)
    return jnp.where(imag, -sign * lane_roll(a, 8), sign * lane_roll(a, -8))


def body_kernel(
    x_ref, out_ref, log_ref,
    own, yf, o_buf, g_buf, l_buf, xb, lhs, s_buf, spec, acc, fb, rb,
    ss_z, rs_z, ss_l, rs_l, ss_o, rs_o, ss_a, rs_a, ss_x, rs_x, ss_f, rs_f,
):
    b, o = lax.axis_index("blk"), lax.axis_index("off")
    x, y, z_lo = b % 4, b // 4 % 4, b // 16
    z_hi, c = o // 2, o % 2
    z = z_hi * 8 + z_lo
    along, across = x * (1 - c) + y * c, y * (1 - c) + x * c

    def device(dx, dy, dz, core):
        zz = (z + dz) % 16
        return (zz % 8 * 16 + (y + dy) % 4 * 4 + (x + dx) % 4, zz // 8 * 2 + core)

    def along_peer(d):
        return device(d * (1 - c), d * c, 0, c)

    def across_peer(d, core):
        return device(d * c, d * (1 - c), 0, core)

    def remote(src, dst, send, recv, to):
        return pltpu.make_async_remote_copy(
            src_ref=src, dst_ref=dst, send_sem=send, recv_sem=recv,
            device_id=to, device_id_type=MESH,
        )

    partner = device(0, 0, 0, 1 - c)
    barrier = pltpu.get_barrier_semaphore()
    peers = [partner] + [device(0, 0, d, c) for d in (-2, -1, 1, 2)]
    for d in (1, 2, 3):
        for core in (0, 1):
            peers += [device(d, 0, 0, core), device(0, d, 0, core)]
    for peer in peers:
        pl.semaphore_signal(barrier, inc=1, device_id=peer, device_id_type=MESH)

    place = iota((128, 128), 1)
    source = place // 8 % 2 * 64 + place // 16 * 8 + place % 8
    permute = jnp.where(iota((128, 128), 0) == source, 1.0, 0.0).astype(bf16)
    yf[...] = nn(x_ref[...].astype(f32).reshape(128, 128).astype(bf16), permute)
    rows = [yf[pl.ds(r, 16, stride=8), :] for r in range(8)]
    for bit in (1, 2, 4):
        upper = lane_bit((16, 128), 16 * bit)
        for r in range(8):
            if r & bit == 0:
                low, high = rows[r], rows[r | bit]
                rows[r] = jnp.where(upper, lane_roll(high, 16 * bit), low)
                rows[r | bit] = jnp.where(upper, high, lane_roll(low, -16 * bit))
    for k in range(8):
        tile = rows[k].astype(bf16)
        own[k] = tile
        g_buf[0, 0, k, along] = tile
        o_buf[0, c, k] = tile

    pl.semaphore_wait(barrier, len(peers))

    sends = []

    def go(copy):
        copy.start()
        sends.append(copy)
        return copy

    def z_copy(src, h, plane, dz):
        return remote(src, g_buf.at[h, plane, :, along], ss_z.at[h, plane], rs_z.at[h, plane], device(0, 0, dz, c))

    def l_copy(src, n):
        return remote(src, l_buf.at[n], ss_l.at[n], rs_l.at[n], device(0, 0, 2, c))

    def o_copy(src, h, path):
        return remote(src, o_buf.at[h, path], ss_o.at[h], rs_o.at[h], partner)

    def a_copy(h, plane, d, place):
        return remote(
            g_buf.at[h, plane, :, place], g_buf.at[h, plane, :, place],
            ss_a.at[h, plane, d - 1], rs_a.at[h, plane, d - 1], along_peer(d),
        )

    def send_along(h, plane):
        for d in (1, 2, 3):
            go(a_copy(h, plane, d, along))

    def wait_along(h):
        for plane in (2, 1, 0):
            for d in (1, 2, 3):
                a_copy(h, plane, d, (along + 4 - d) % 4).wait_recv()

    def plane_of(a, d):
        mine = (4 * across + a) * (1 - c) + (4 * a + across) * c
        theirs_across = (across + d) % 4
        theirs = (4 * theirs_across + along) * (1 - c) + (4 * along + theirs_across) * c
        return (theirs - mine + 15) // 16 * 2

    def half_of(h, plane):
        return (h + (z_lo + plane) // 8) % 2

    def send_across(h):
        def to_first(d):
            return remote(
                g_buf.at[h, 1], xb.at[half_of(h, 1), c, :, across],
                ss_x.at[h, d], rs_x.at[h, c, d], across_peer(d, 0),
            )

        def to_second(d, a):
            plane = plane_of(a, d)
            return remote(
                g_buf.at[h, plane, :, a], xb.at[half_of(h, plane), c, :, across, a],
                ss_x.at[h, d], rs_x.at[h, c, d], across_peer(d, 1),
            )

        for d in (1, 3, 2):
            to_first(d).start()
            for a in range(4):
                to_second(d, a).start()

        @pl.when(c == 0)
        def _():
            for a in range(4):
                to_second(0, a).start()
            pltpu.make_async_copy(
                g_buf.at[h, 1], xb.at[half_of(h, 1), c, :, across], rs_x.at[h, c, 0]
            ).start()

        @pl.when(c == 1)
        def _():
            to_first(0).start()
            for a in range(4):
                plane = plane_of(a, 0)
                pltpu.make_async_copy(
                    g_buf.at[h, plane, :, a], xb.at[half_of(h, plane), c, :, across, a], rs_x.at[h, c, 0]
                ).start()

    def wait_across(h):
        for path, mid in ((0, y), (1, x)):
            for d in range(4):
                place = (mid + 4 - d) % 4
                region = xb.at[h, path, :, place]
                pltpu.make_async_copy(region, region, rs_x.at[h, path, d]).wait()

    go(l_copy(own, 0))
    go(z_copy(own, 0, 2, -2))
    go(z_copy(own, 0, 1, -1))
    go(o_copy(own, 0, c))
    send_along(0, 0)

    def frequency_of(q):
        k, u = q // 16, q % 8
        return 8 * k + (k - u + 8) % 8, q // 8 % 2

    def table(q_dim):
        q, s = iota((128, 128), q_dim), iota((128, 128), 1 - q_dim)
        m, part = frequency_of(q)
        phase = (m * s % 128).astype(f32) * (2.0 * math.pi / 128)
        return jnp.where(part == 0, jnp.cos(phase), -jnp.sin(phase))

    f_high, f_low = split(table(1))
    forward = jnp.concatenate([f_high, f_high, f_low], axis=1)
    b_high, b_low = split(table(0))
    backward = jnp.concatenate([b_high, b_high, b_low], axis=1)

    def matches(k):
        u, t = iota((8, 128), 0), iota((8, 128), 1) % 8
        return (u + t) % 8 == k

    def build_lhs(h):
        squares = jnp.zeros((8, 128), f32)
        for path in (0, 1):
            for k in range(8):
                both = o_buf[h, path, k].astype(f32)
                rows = jnp.where(z_hi == 0, both[:8], both[8:])
                squares = squares + rows * rows
                turned = rotate_parts(rows, 1.0)
                pair = [jnp.where(matches(k)[None], v[:, None, :], 0.0) for v in (rows, turned)]
                block = jnp.concatenate(pair, axis=1).reshape(128, 128)
                lhs[h, k, :, path * 128 : path * 128 + 128] = block.astype(bf16)
        return squares

    def tile_of(h, path, k):
        if path == 0:
            return xb[h, 0, k].reshape(256, 128)
        return jnp.concatenate([xb[h, 1, k, a, bb] for bb in range(4) for a in range(4)], axis=0)

    def cross(squares):
        for k in range(8):
            tiles = [tile_of(h, path, k) for h in (0, 1) for path in (0, 1)]
            for t in tiles:
                wide = t.astype(f32)
                squares = squares + wide * wide
            left = jnp.concatenate([lhs[0, k], lhs[1, k]], axis=1)
            s_buf[k] = nt(left, jnp.concatenate(tiles, axis=1))
        return squares

    l_copy(own, 0).wait_recv()
    go(l_copy(l_buf.at[0], 1))
    z_copy(own, 0, 1, -1).wait_recv()
    send_along(0, 1)
    z_copy(own, 0, 2, -2).wait_recv()
    send_along(0, 2)
    l_copy(own, 1).wait_recv()
    go(z_copy(l_buf.at[1], 1, 2, 2))
    wait_along(0)
    send_across(0)
    z_copy(own, 1, 2, 2).wait_recv()
    go(z_copy(g_buf.at[1, 2, :, along], 1, 0, 2))
    go(z_copy(g_buf.at[1, 2, :, along], 1, 1, 1))
    send_along(1, 2)
    o_copy(own, 0, 1 - c).wait_recv()
    own_squares = build_lhs(0)
    z_copy(own, 1, 1, 1).wait_recv()
    send_along(1, 1)
    z_copy(own, 1, 0, 2).wait_recv()
    send_along(1, 0)
    go(o_copy(g_buf.at[1, 0, :, along], 1, c))
    for k in range(8):
        o_buf[1, c, k] = g_buf[1, 0, k, along]
    wait_across(0)
    wait_along(1)
    send_across(1)
    o_copy(own, 1, 1 - c).wait_recv()
    own_squares = own_squares + build_lhs(1)
    wait_across(1)
    squares = cross(jnp.zeros((256, 128), f32))

    def pieces(a):
        high, low = split(a)
        rest = (a - high.astype(f32) - low.astype(f32)).astype(bf16)
        return [high, low, rest]

    ones = jnp.ones((8, 384), bf16)
    norm_squares = nt(ones, jnp.concatenate(pieces(squares), axis=1))
    own_norm = jnp.sum(own_squares, axis=1, keepdims=True)
    gain = lax.rsqrt(norm_squares + epsilon) * (concentration * lax.rsqrt(own_norm + epsilon))

    lane = iota((128, 256), 1)
    own_lane = jnp.where(c == 1, (y * 4 + x) * 16 + z_hi * 8, -1000)
    for i in range(8):
        s_i = jnp.concatenate([s_buf[k, i * 16 : i * 16 + 16, :] for k in range(8)], axis=0)
        high, low = split(s_i)
        correlation = nn(forward, jnp.concatenate([high, low, high], axis=0))
        weights = jnp.exp(correlation * gain[i : i + 1])
        weights = jnp.where(lane == own_lane + i, 0.0, weights)
        high, low = split(weights)
        spectral = nn(backward, jnp.concatenate([high, low, high], axis=0))
        degree = jnp.sum(spectral[0:1], axis=1, keepdims=True)
        fb[i, 4] = jnp.broadcast_to(degree, (8, 128))
        rounded = spectral.astype(bf16)
        for k in range(8):
            spec[k, i * 16 : i * 16 + 16, :] = rounded[k * 16 : k * 16 + 16]

    for k in range(8):
        keep = jnp.concatenate([matches(k)] * 16, axis=0)
        for h in (0, 1):
            for path in (0, 1):
                part = nn(spec[k], tile_of(h, path, k))
                n = 2 * h + path
                acc[n] = part if k == 0 else jnp.where(keep, part, acc[n])
    for n in range(4):
        pair = acc[n].reshape(8, 16, 128)
        total = pair[:, :8] + rotate_parts(pair[:, 8:], -1.0)
        for i in range(8):
            fb[i, n] = total[i]

    last = remote(fb.at[pl.ds((1 - c) * 4, 4)], rb, ss_f, rs_f, partner)
    last.start()
    last.wait()
    total = fb[pl.ds(c * 4, 4)] + rb[...]
    degree = total[:, 4:5]
    v = (total[:, :4] / degree).reshape(16, 8, 128)
    for bit in (1, 2, 4):
        v = jnp.where(lane_bit(v.shape, bit), pltpu.roll(v, bit, 1), v)
    for bit in (1, 2, 4):
        group = lane_bit(v.shape, 16 * bit)
        row = iota(v.shape, 1) // bit % 2 == 1
        down = lane_roll(pltpu.roll(v, 8 - bit, 1), 16 * bit)
        up = lane_roll(pltpu.roll(v, bit, 1), -16 * bit)
        v = jnp.where(group == row, v, jnp.where(group, down, up))
    flat = sum(nt(p, permute) for p in pieces(v.reshape(128, 128)))
    flat = flat.reshape(4, 4, 8, 128)
    for h in (0, 1):
        for path in (0, 1):
            start = pl.multiple_of(((z_hi + h) % 2 * 2 + path) * 8, 8)
            out_ref[:, pl.ds(start, 8), :] = flat[:, 2 * h + path]
    logs = jnp.log(degree[:, 0])
    pick = iota((8, 128), 1)
    line = jnp.zeros((8, 128), f32)
    for i in range(4):
        line = jnp.where(pick == i, logs[i], line)
    log_ref[...] = line

    for copy in sends:
        copy.wait_send()
    for h in (0, 1):
        for d in (1, 2, 3):
            both = g_buf.at[h, pl.ds(0, 2)]
            remote(both, both, ss_x.at[h, d], rs_x.at[h, 0, d], partner).wait_send()
        one = g_buf.at[h, 0]
        remote(one, one, ss_x.at[h, 0], rs_x.at[h, 0, 0], partner).wait_send()


def body(coefficients):
    vmem = pl.BlockSpec(memory_space=pltpu.VMEM)
    dma = pltpu.SemaphoreType.DMA
    smoothed, logs = pl.pallas_call(
        body_kernel,
        out_shape=(
            jax.ShapeDtypeStruct((4, 32, 128), f32),
            jax.ShapeDtypeStruct((8, 128), f32),
        ),
        in_specs=[vmem],
        out_specs=(vmem, vmem),
        scratch_shapes=[
            pltpu.VMEM((8, 16, 128), bf16),
            pltpu.VMEM((128, 128), f32),
            pltpu.VMEM((2, 2, 8, 16, 128), bf16),
            pltpu.VMEM((2, 3, 8, 4, 16, 128), bf16),
            pltpu.VMEM((2, 8, 16, 128), bf16),
            pltpu.VMEM((2, 2, 8, 4, 4, 16, 128), bf16),
            pltpu.VMEM((2, 8, 128, 256), bf16),
            pltpu.VMEM((8, 128, 256), f32),
            pltpu.VMEM((8, 128, 256), bf16),
            pltpu.VMEM((4, 128, 128), f32),
            pltpu.VMEM((8, 5, 8, 128), f32),
            pltpu.VMEM((4, 5, 8, 128), f32),
            dma((2, 3)), dma((2, 3)),
            dma((2,)), dma((2,)),
            dma((2,)), dma((2,)),
            dma((2, 3, 3)), dma((2, 3, 3)),
            dma((2, 4)), dma((2, 2, 4)),
            dma, dma,
        ],
        compiler_params=pltpu.CompilerParams(collective_id=0, has_side_effects=True),
        name="graph_filter",
    )(coefficients)
    return smoothed, logs[0, :4]


def solution(mesh):
    return jax.shard_map(
        body,
        mesh=mesh,
        in_specs=(P("blk", "off", None),),
        out_specs=(P(("blk", "off"), None, None), P(("blk", "off"))),
        check_vma=False,
    )
```

```python
import functools
import functools
import math

import jax
import jax.numpy as jnp
from jax import lax
from jax.experimental import pallas as pl
from jax.experimental.pallas import tpu as pltpu
from jax.sharding import PartitionSpec as P

MESH = pl.DeviceIdType.MESH
epsilon = 1e-06
concentration = 40.0
f32, bf16 = jnp.float32, jnp.bfloat16


def nt(a, b):
    return lax.dot_general(a, b, (((1,), (1,)), ((), ())), preferred_element_type=f32)


def nn(a, b):
    return jnp.dot(a, b, preferred_element_type=f32)


def split(a):
    high = a.astype(bf16)
    return high, (a - high.astype(f32)).astype(bf16)


def iota(shape, dim):
    return lax.broadcasted_iota(jnp.int32, shape, dim)


def lane_bit(shape, bit):
    return iota(shape, len(shape) - 1) // bit % 2 == 1


def lane_roll(a, by):
    return pltpu.roll(a, by % 128, a.ndim - 1)


def rotate_parts(a, sign):
    imag = lane_bit(a.shape, 8)
    return jnp.where(imag, -sign * lane_roll(a, 8), sign * lane_roll(a, -8))


places = [
    (0, 0), (0, 1), (1, 0), (0, 3), (3, 0), (0, 2), (2, 0), (1, 1),
    (1, 3), (3, 1), (3, 3), (1, 2), (2, 1), (3, 2), (2, 3), (2, 2),
]
slot_of = {place: n for n, place in enumerate(places)}


def body_kernel(
    x_ref, out_ref, log_ref,
    x_buf, yf, o_buf, g_buf, xb, lhs, s_buf, sq_buf, spec, acc, fb, rb,
    x_sem, ss_z, rs_z, ss_o, rs_o, ss_far, rs_far, ok_sem, ss_a, rs_a, ss_x, rs_x, ss_f, rs_f,
):
    b, o = lax.axis_index("blk"), lax.axis_index("off")
    x, y, z_lo = b % 4, b // 4 % 4, b // 16
    z_hi, c = o // 2, o % 2
    z = z_hi * 8 + z_lo

    load = pltpu.make_async_copy(x_ref, x_buf, x_sem)
    load.start()

    def device(dx, dy, dz, core):
        zz = (z + dz) % 16
        return (zz % 8 * 16 + (y + dy) % 4 * 4 + (x + dx) % 4, zz // 8 * 2 + core)

    def remote(src, dst, send, recv, to):
        return pltpu.make_async_remote_copy(
            src_ref=src, dst_ref=dst, send_sem=send, recv_sem=recv,
            device_id=to, device_id_type=MESH,
        )

    partner = device(0, 0, 0, 1 - c)
    opposite = device(0, 0, 8, c)
    barrier = pltpu.get_barrier_semaphore()
    peers = [partner] + [device(0, 0, d, c) for d in (-2, -1, 1, 2)]
    for d in (1, 3, 2):
        for core in (0, 1):
            peers += [device(d, 0, 0, core), device(0, d, 0, core)]

    def announce(peer):
        pl.semaphore_signal(barrier, inc=1, device_id=peer, device_id_type=MESH)

    @pl.when(z_hi == 0)
    def _():
        announce(opposite)

    for peer in peers:
        announce(peer)

    place = iota((128, 128), 1)
    source = place // 8 % 2 * 64 + place // 16 * 8 + place % 8
    permute = jnp.where(iota((128, 128), 0) == source, 1.0, 0.0).astype(bf16)
    load.wait()
    yf[...] = nn(x_buf[...].astype(f32).reshape(128, 128).astype(bf16), permute)
    rows = [yf[pl.ds(r, 16, stride=8), :] for r in range(8)]
    for bit in (1, 2, 4):
        upper = lane_bit((16, 128), 16 * bit)
        for r in range(8):
            if r & bit == 0:
                low, high = rows[r], rows[r | bit]
                rows[r] = jnp.where(upper, lane_roll(high, 16 * bit), low)
                rows[r | bit] = jnp.where(upper, high, lane_roll(low, -16 * bit))
    for k in range(8):
        tile = rows[k].astype(bf16)
        g_buf[0, 0, 0, k] = tile
        o_buf[0, c, k] = tile

    pl.semaphore_wait(barrier, len(peers) + z_hi)

    own = g_buf.at[0, 0, 0]
    far_own = g_buf.at[1, 0, 0]

    far_copy = remote(own, far_own, ss_far, rs_far, opposite)

    @pl.when(z_hi == 1)
    def _():
        far_copy.start()
        pl.semaphore_signal(ok_sem, inc=1, device_id=opposite, device_id_type=MESH)

    def z_copy(h, plane):
        return remote(
            g_buf.at[h, 0, 0], g_buf.at[h, plane, 0], ss_z.at[h, plane], rs_z.at[h, plane], device(0, 0, -plane, c)
        )

    def o_copy(h, path):
        return remote(g_buf.at[h, 0, 0], o_buf.at[h, path], ss_o.at[h], rs_o.at[h], partner)

    def half_of(h, plane):
        return (h + (z_lo + plane) // 8) % 2

    def a_copy(h, plane, j):
        return remote(
            g_buf.at[h, plane, 0], g_buf.at[h, plane, j],
            ss_a.at[h, plane, j - 1], rs_a.at[h, plane, j - 1], device(-j * (1 - c), -j * c, 0, c),
        )

    def send_along(h, plane):
        for j in (2, 1, 3):
            a_copy(h, plane, j).start()

    def plane_of(j, d):
        first = (4 * ((y + d) % 4) + x) - (4 * y + (x + j) % 4)
        second = (4 * y + (x + d) % 4) - (4 * ((y + j) % 4) + x)
        return (first * (1 - c) + second * c + 15) // 16 * 2

    def slot(j, d):
        return slot_of[j, -d % 4] * (1 - c) + slot_of[-d % 4, j] * c

    def x_copy(h, plane, j, d, core):
        n = slot(j, d)
        lot = 2 if d == 0 else d // 3
        return remote(
            g_buf.at[h, plane, j], xb.at[half_of(h, plane), c, n],
            ss_x.at[h, core, lot], rs_x.at[h, n // 8], device(d * c, d * (1 - c), 0, core),
        )

    def keep_copy(h, plane, j):
        n = slot(j, 0)
        return pltpu.make_async_copy(
            g_buf.at[h, plane, j], xb.at[half_of(h, plane), c, n], rs_x.at[h, n // 8]
        )

    def send_across(h, plane, j):
        core = 0 if plane == 1 else 1

        def when(d, *more):
            wanted = [] if plane == 1 else [plane_of(j, d) == plane]
            tests = wanted + list(more)
            if not tests:
                return lambda f: f()
            return pl.when(functools.reduce(jnp.logical_and, tests))

        for d in (2, 1, 3):
            when(d)(lambda d=d: x_copy(h, plane, j, d, core).start())
        when(0, c != core)(lambda: x_copy(h, plane, j, 0, core).start())
        when(0, c == core)(lambda: keep_copy(h, plane, j).start())

    def relay(h, plane, j):
        a_copy(h, plane, j).wait_recv()
        send_across(h, plane, j)

    def wait_slots(h, group):
        region = xb.at[0, :, pl.ds(group * 8, 8)]
        pltpu.make_async_copy(region, region, rs_x.at[h, group]).wait()

    def spread(h):
        z_copy(h, 2).start()
        z_copy(h, 1).start()
        o_copy(h, c).start()
        send_along(h, 0)
        send_across(h, 0, 0)

    spread(0)

    def frequency_of(q):
        k, u = q // 16, q % 8
        return 8 * k + (k - u + 8) % 8, q // 8 % 2

    def table(q_dim):
        q, s = iota((128, 128), q_dim), iota((128, 128), 1 - q_dim)
        m, part = frequency_of(q)
        phase = (m * s % 128).astype(f32) * (2.0 * math.pi / 128)
        return jnp.where(part == 0, jnp.cos(phase), -jnp.sin(phase))

    f_high, f_low = split(table(1))
    forward = jnp.concatenate([f_high, f_high, f_low], axis=1)
    b_high, b_low = split(table(0))
    backward = jnp.concatenate([b_high, b_high, b_low], axis=1)

    def matches(k):
        u, t = iota((8, 128), 0), iota((8, 128), 1) % 8
        return (u + t) % 8 == k

    def build_lhs(h):
        squares = jnp.zeros((8, 128), f32)
        for path in (0, 1):
            for k in range(8):
                both = o_buf[h, path, k].astype(f32)
                rows = jnp.where(z_hi == 0, both[:8], both[8:])
                squares = squares + rows * rows
                turned = rotate_parts(rows, 1.0)
                pair = [jnp.where(matches(k)[None], v[:, None, :], 0.0) for v in (rows, turned)]
                block = jnp.concatenate(pair, axis=1).reshape(128, 128)
                lhs[h, k, :, path * 128 : path * 128 + 128] = block.astype(bf16)
        return squares

    def tile_of(h, path, k, group):
        return xb[h, path, group * 8 : group * 8 + 8, k].reshape(128, 128)

    def cross(halves, group, first):
        squares = jnp.zeros((128, 128), f32) if first else sq_buf[group]
        for k in range(8):
            tiles = [tile_of(h, path, k, group) for h in halves for path in (0, 1)]
            for t in tiles:
                wide = t.astype(f32)
                squares = squares + wide * wide
            left = jnp.concatenate([lhs[h, k] for h in halves], axis=1)
            part = nt(left, jnp.concatenate(tiles, axis=1))
            s_buf[group, k] = part if first else s_buf[group, k] + part
        sq_buf[group] = squares

    def pieces(a):
        high, low = split(a)
        rest = (a - high.astype(f32) - low.astype(f32)).astype(bf16)
        return [high, low, rest]

    def forward_planes(h):
        z_copy(h, 1).wait_recv()
        send_along(h, 1)
        send_across(h, 1, 0)
        z_copy(h, 2).wait_recv()
        send_along(h, 2)
        send_across(h, 2, 0)
        for plane in (0, 1, 2):
            for j in (1, 3, 2):
                relay(h, plane, j)

    forward_planes(0)

    @pl.when(z_hi == 0)
    def _():
        pl.semaphore_wait(ok_sem, 1)
        far_copy.start()

    o_copy(0, 1 - c).wait_recv()
    own_squares = build_lhs(0)
    far_copy.wait_recv()
    spread(1)
    for k in range(8):
        o_buf[1, c, k] = g_buf[1, 0, 0, k]
    forward_planes(1)
    o_copy(1, 1 - c).wait_recv()
    own_squares = own_squares + build_lhs(1)
    own_gain = concentration * lax.rsqrt(jnp.sum(own_squares, axis=1, keepdims=True) + epsilon)

    early = z_lo < 6
    for group in (0, 1):
        wait_slots(0, group)

    @pl.when(early)
    def _():
        for group in (0, 1):
            cross((0,), group, True)

    ones = jnp.ones((8, 384), bf16)
    lane = iota((128, 256), 1)
    own_lane = z_hi * 8 - 1000 * (1 - c)

    def filter_group(group):
        norm_squares = nt(ones, jnp.concatenate(pieces(sq_buf[group]), axis=1))
        gain = lax.rsqrt(norm_squares + epsilon) * own_gain
        for i in (0, 2, 4, 6):
            two = [
                jnp.concatenate([s_buf[group, k, ii * 16 : ii * 16 + 16, :] for k in range(8)], axis=0)
                for ii in (i, i + 1)
            ]
            high, low = split(jnp.concatenate(two, axis=1))
            correlation = nn(forward, jnp.concatenate([high, low, high], axis=0))
            scale = jnp.concatenate([gain[i : i + 1], gain[i + 1 : i + 2]], axis=1)
            weights = jnp.exp(correlation * scale)
            if group == 0:
                same = lane - jnp.where(lane >= 128, 129, 0) == own_lane + i
                weights = jnp.where(same, 0.0, weights)
            high, low = split(weights)
            spectral = nn(backward, jnp.concatenate([high, low, high], axis=0))
            rounded = spectral.astype(bf16)
            for ii in (0, 1):
                part = spectral[:, ii * 128 : ii * 128 + 128]
                degree = jnp.broadcast_to(jnp.sum(part[0:1], axis=1, keepdims=True), (8, 128))
                fb[i + ii, 4] = degree if group == 0 else fb[i + ii, 4] + degree
                for k in range(8):
                    spec[k, (i + ii) * 16 : (i + ii) * 16 + 16, :] = rounded[
                        k * 16 : k * 16 + 16, ii * 128 : ii * 128 + 128
                    ]
        for k in range(8):
            keep = jnp.concatenate([matches(k)] * 16, axis=0)
            for h in (0, 1):
                for path in (0, 1):
                    part = nn(spec[k], tile_of(h, path, k, group))
                    n = 2 * h + path
                    if group == 0:
                        acc[n] = part if k == 0 else jnp.where(keep, part, acc[n])
                    else:
                        acc[n] = acc[n] + jnp.where(keep, part, 0.0)

    for group in (0, 1):
        wait_slots(1, group)

        @pl.when(early)
        def _():
            cross((1,), group, False)

        @pl.when(jnp.logical_not(early))
        def _():
            cross((0, 1), group, True)

        filter_group(group)

    for n in range(4):
        pair = acc[n].reshape(8, 16, 128)
        total = pair[:, :8] + rotate_parts(pair[:, 8:], -1.0)
        for i in range(8):
            fb[i, n] = total[i]

    last = remote(fb.at[pl.ds((1 - c) * 4, 4)], rb, ss_f, rs_f, partner)
    last.start()
    last.wait()
    total = fb[pl.ds(c * 4, 4)] + rb[...]
    degree = total[:, 4:5]
    v = (total[:, :4] / degree).reshape(16, 8, 128)
    for bit in (1, 2, 4):
        v = jnp.where(lane_bit(v.shape, bit), pltpu.roll(v, bit, 1), v)
    for bit in (1, 2, 4):
        group = lane_bit(v.shape, 16 * bit)
        row = iota(v.shape, 1) // bit % 2 == 1
        down = lane_roll(pltpu.roll(v, 8 - bit, 1), 16 * bit)
        up = lane_roll(pltpu.roll(v, bit, 1), -16 * bit)
        v = jnp.where(group == row, v, jnp.where(group, down, up))
    flat = sum(nt(p, permute) for p in pieces(v.reshape(128, 128)))
    flat = flat.reshape(4, 4, 8, 128)
    for h in (0, 1):
        for path in (0, 1):
            start = pl.multiple_of(((z_hi + h) % 2 * 2 + path) * 8, 8)
            out_ref[:, pl.ds(start, 8), :] = flat[:, 2 * h + path]
    logs = jnp.log(degree[:, 0])
    pick = iota((8, 128), 1)
    line = jnp.zeros((8, 128), f32)
    for i in range(4):
        line = jnp.where(pick == i, logs[i], line)
    log_ref[...] = line

    far_copy.wait_send()
    for h in (0, 1):
        z_copy(h, 1).wait_send()
        z_copy(h, 2).wait_send()
        o_copy(h, c).wait_send()
        for plane in (0, 1, 2):
            for j in (1, 2, 3):
                a_copy(h, plane, j).wait_send()
        for core in (0, 1):
            for lot, count in enumerate((8, 4)):
                sent = xb.at[0, 0, pl.ds(0, count)]
                remote(sent, sent, ss_x.at[h, core, lot], rs_x.at[h, 0], partner).wait_send()

        def sent_over(core):
            sent = xb.at[0, 0, pl.ds(0, 4)]
            remote(sent, sent, ss_x.at[h, core, 2], rs_x.at[h, 0], partner).wait_send()

        pl.when(c == 0)(functools.partial(sent_over, 1))
        pl.when(c == 1)(functools.partial(sent_over, 0))


def body(coefficients):
    vmem = pl.BlockSpec(memory_space=pltpu.VMEM)
    dma = pltpu.SemaphoreType.DMA
    smoothed, logs = pl.pallas_call(
        body_kernel,
        out_shape=(
            jax.ShapeDtypeStruct((4, 32, 128), f32),
            jax.ShapeDtypeStruct((8, 128), f32),
        ),
        in_specs=[pl.BlockSpec(memory_space=pl.ANY)],
        out_specs=(vmem, vmem),
        scratch_shapes=[
            pltpu.VMEM((16, 8, 128), bf16),
            pltpu.VMEM((128, 128), f32),
            pltpu.VMEM((2, 2, 8, 16, 128), bf16),
            pltpu.VMEM((2, 3, 4, 8, 16, 128), bf16),
            pltpu.VMEM((2, 2, 16, 8, 16, 128), bf16),
            pltpu.VMEM((2, 8, 128, 256), bf16),
            pltpu.VMEM((2, 8, 128, 128), f32),
            pltpu.VMEM((2, 128, 128), f32),
            pltpu.VMEM((8, 128, 128), bf16),
            pltpu.VMEM((4, 128, 128), f32),
            pltpu.VMEM((8, 5, 8, 128), f32),
            pltpu.VMEM((4, 5, 8, 128), f32),
            dma,
            dma((2, 3)), dma((2, 3)),
            dma((2,)), dma((2,)),
            dma, dma,
            pltpu.SemaphoreType.REGULAR,
            dma((2, 3, 3)), dma((2, 3, 3)),
            dma((2, 2, 3)), dma((2, 2)),
            dma, dma,
        ],
        compiler_params=pltpu.CompilerParams(collective_id=0, has_side_effects=True),
        name="graph_filter",
    )(coefficients)
    return smoothed, logs[0, :4]


def solution(mesh):
    return jax.shard_map(
        body,
        mesh=mesh,
        in_specs=(P("blk", "off", None),),
        out_specs=(P(("blk", "off"), None, None), P(("blk", "off"))),
        check_vma=False,
    )
```

```python
import functools
import functools
import math

import jax
import jax.numpy as jnp
from jax import lax
from jax.experimental import pallas as pl
from jax.experimental.pallas import tpu as pltpu
from jax.sharding import PartitionSpec as P

MESH = pl.DeviceIdType.MESH
epsilon = 1e-06
concentration = 40.0
f32, bf16 = jnp.float32, jnp.bfloat16


def nt(a, b):
    return lax.dot_general(a, b, (((1,), (1,)), ((), ())), preferred_element_type=f32)


def nn(a, b):
    return jnp.dot(a, b, preferred_element_type=f32)


def split(a):
    high = a.astype(bf16)
    return high, (a - high.astype(f32)).astype(bf16)


def iota(shape, dim):
    return lax.broadcasted_iota(jnp.int32, shape, dim)


def lane_bit(shape, bit):
    return iota(shape, len(shape) - 1) // bit % 2 == 1


def lane_roll(a, by):
    return pltpu.roll(a, by % 128, a.ndim - 1)


def permutation():
    place = iota((128, 128), 1)
    source = place // 8 % 2 * 64 + place // 16 * 8 + place % 8
    return jnp.where(iota((128, 128), 0) == source, 1.0, 0.0).astype(bf16)


def pieces(a):
    high, low = split(a)
    return [high, low, (a - high.astype(f32) - low.astype(f32)).astype(bf16)]


def rotate_parts(a, sign):
    imag = lane_bit(a.shape, 8)
    return jnp.where(imag, -sign * lane_roll(a, 8), sign * lane_roll(a, -8))


places = [
    (0, 0), (0, 1), (1, 0), (0, 3), (3, 0), (0, 2), (2, 0), (1, 1),
    (1, 3), (3, 1), (3, 3), (1, 2), (2, 1), (3, 2), (2, 3), (2, 2),
]
slot_of = {place: n for n, place in enumerate(places)}


def body_kernel(
    x_ref, out_ref,
    x_buf, yf, o_buf, g_buf, xb, lhs, s_buf, sq_buf, spec, acc, fb, rb,
    x_sem, ss_z, rs_z, ss_o, rs_o, ss_far, rs_far, ok_sem, wrap_sem, ss_a, rs_a, ss_x, rs_x, ss_f, rs_f,
):
    b, o = lax.axis_index("blk"), lax.axis_index("off")
    x, y, z_lo = b % 4, b // 4 % 4, b // 16
    z_hi, c = o // 2, o % 2
    z = z_hi * 8 + z_lo

    load = pltpu.make_async_copy(x_ref, x_buf, x_sem)
    load.start()

    def device(dx, dy, dz, core):
        zz = (z + dz) % 16
        return (zz % 8 * 16 + (y + dy) % 4 * 4 + (x + dx) % 4, zz // 8 * 2 + core)

    def remote(src, dst, send, recv, to):
        return pltpu.make_async_remote_copy(
            src_ref=src, dst_ref=dst, send_sem=send, recv_sem=recv,
            device_id=to, device_id_type=MESH,
        )

    partner = device(0, 0, 0, 1 - c)
    opposite = device(0, 0, 8, c)
    barrier = pltpu.get_barrier_semaphore()
    peers = [partner]
    for d in (1, 3, 2):
        for core in (0, 1):
            peers += [device(d, 0, 0, core), device(0, d, 0, core)]

    def announce(peer):
        pl.semaphore_signal(barrier, inc=1, device_id=peer, device_id_type=MESH)

    @pl.when(z_hi == 0)
    def _():
        announce(opposite)

    for peer in peers:
        announce(peer)

    late = (z + 2) // 16 + (z + 1) // 16
    first = (z + 15) // 16 + (z + 14) // 16
    for d in (1, 2):
        crossing = (z + d) // 16 == 1
        pl.when(jnp.logical_not(crossing))(lambda d=d: announce(device(0, 0, d, c)))
        pl.when(z - d < 0)(lambda d=d: announce(device(0, 0, -d, c)))

    permute = permutation()
    load.wait()
    yf[...] = nn(x_buf[...].astype(f32).reshape(128, 128).astype(bf16), permute)
    rows = [yf[pl.ds(r, 16, stride=8), :] for r in range(8)]
    for bit in (1, 2, 4):
        upper = lane_bit((16, 128), 16 * bit)
        for r in range(8):
            if r & bit == 0:
                low, high = rows[r], rows[r | bit]
                rows[r] = jnp.where(upper, lane_roll(high, 16 * bit), low)
                rows[r | bit] = jnp.where(upper, high, lane_roll(low, -16 * bit))
    for k in range(8):
        tile = rows[k].astype(bf16)
        g_buf[0, 0, 0, k] = tile
        o_buf[0, c, k] = tile

    pl.semaphore_wait(barrier, len(peers) + z_hi + late + first)
    for d in (1, 2):
        @pl.when((z + d) // 16 == 1)
        def _():
            pl.semaphore_signal(
                wrap_sem, inc=1, device_id=device(0, 0, d, c), device_id_type=MESH
            )

    own = g_buf.at[0, 0, 0]
    far_own = g_buf.at[1, 0, 0]

    def cut(ref, part):
        return ref if part is None else ref.at[pl.ds(4 * part, 4)]

    def far_copy(part):
        return remote(cut(own, part), cut(far_own, part), ss_far.at[part], rs_far.at[part], opposite)

    @pl.when(z_hi == 1)
    def _():
        far_copy(0).start()
        far_copy(1).start()
        pl.semaphore_signal(ok_sem, inc=1, device_id=opposite, device_id_type=MESH)

    def z_copy(h, plane, part=None):
        n = part or 0
        return remote(
            cut(g_buf.at[h, 0, 0], part), cut(g_buf.at[h, plane, 0], part),
            ss_z.at[h, plane, n], rs_z.at[h, plane, n], device(0, 0, -plane, c),
        )

    def o_copy(h, path):
        return remote(g_buf.at[h, 0, 0], o_buf.at[h, path], ss_o.at[h], rs_o.at[h], partner)

    def half_of(h, plane):
        return (h + (z_lo + plane) // 8) % 2

    def a_copy(h, plane, j, part):
        n = part or 0
        return remote(
            cut(g_buf.at[h, plane, 0], part), cut(g_buf.at[h, plane, j], part),
            ss_a.at[h, plane, j - 1, n], rs_a.at[h, plane, j - 1, n], device(-j * (1 - c), -j * c, 0, c),
        )

    def send_along(h, plane, part):
        for j in (2, 1, 3):
            a_copy(h, plane, j, part).start()

    def plane_of(j, d):
        first = (4 * ((y + d) % 4) + x) - (4 * y + (x + j) % 4)
        second = (4 * y + (x + d) % 4) - (4 * ((y + j) % 4) + x)
        return (first * (1 - c) + second * c + 15) // 16 * 2

    def slot(j, d):
        return slot_of[j, -d % 4] * (1 - c) + slot_of[-d % 4, j] * c

    def x_copy(h, plane, j, d, core, part):
        n = slot(j, d)
        lot = 2 if d == 0 else d // 3
        return remote(
            cut(g_buf.at[h, plane, j], part), cut(xb.at[half_of(h, plane), c, n], part),
            ss_x.at[h, core, lot], rs_x.at[h, n // 8], device(d * c, d * (1 - c), 0, core),
        )

    def keep_copy(h, plane, j, part):
        n = slot(j, 0)
        return pltpu.make_async_copy(
            cut(g_buf.at[h, plane, j], part), cut(xb.at[half_of(h, plane), c, n], part), rs_x.at[h, n // 8]
        )

    def send_across(h, plane, j, part):
        core = 0 if plane == 1 else 1

        def when(d, *more):
            wanted = [] if plane == 1 else [plane_of(j, d) == plane]
            tests = wanted + list(more)
            if not tests:
                return lambda f: f()
            return pl.when(functools.reduce(jnp.logical_and, tests))

        for d in (2, 1, 3):
            when(d)(lambda d=d: x_copy(h, plane, j, d, core, part).start())
        when(0, c != core)(lambda: x_copy(h, plane, j, 0, core, part).start())
        when(0, c == core)(lambda: keep_copy(h, plane, j, part).start())

    def wait_slots(h, group):
        region = xb.at[0, :, pl.ds(group * 8, 8)]
        pltpu.make_async_copy(region, region, rs_x.at[h, group]).wait()

    def answer_far():
        @pl.when(z_hi == 0)
        def _():
            pl.semaphore_wait(ok_sem, 1)
            far_copy(0).start()
            far_copy(1).start()

    def spread(h, part):
        if h == 0:
            pl.when(z >= 2)(lambda: z_copy(0, 2).start())
            pl.when(z >= 1)(lambda: z_copy(0, 1).start())
        else:
            z_copy(h, 2, part).start()
            z_copy(h, 1, part).start()
        send_along(h, 0, part)
        send_across(h, 0, 0, part)

    def pass_on(h, plane, part):
        z_copy(h, plane, part).wait_recv()
        send_along(h, plane, part)
        send_across(h, plane, 0, part)

    def relay(h, plane, part):
        for j in (1, 3, 2):
            a_copy(h, plane, j, part).wait_recv()
            send_across(h, plane, j, part)

    o_copy(0, c).start()
    spread(0, None)

    def frequency_of(q):
        k, u = q // 16, q % 8
        return 8 * k + (k - u + 8) % 8, q // 8 % 2

    def table(q_dim):
        q, s = iota((128, 128), q_dim), iota((128, 128), 1 - q_dim)
        m, part = frequency_of(q)
        phase = (m * s % 128).astype(f32) * (2.0 * math.pi / 128)
        return jnp.where(part == 0, jnp.cos(phase), -jnp.sin(phase))

    f_high, f_low = split(table(1))
    forward = jnp.concatenate([f_high, f_high, f_low], axis=1)
    b_high, b_low = split(table(0))
    backward = jnp.concatenate([b_high, b_high, b_low], axis=1)

    def matches(k):
        u, t = iota((8, 128), 0), iota((8, 128), 1) % 8
        return (u + t) % 8 == k

    def build_lhs(h):
        squares = jnp.zeros((8, 128), f32)
        for path in (0, 1):
            for k in range(8):
                both = o_buf[h, path, k].astype(f32)
                rows = jnp.where(z_hi == 0, both[:8], both[8:])
                rows = jnp.where(c == 0, pltpu.roll(rows, 4, 0), rows)
                squares = squares + rows * rows
                turned = rotate_parts(rows, 1.0)
                pair = [jnp.where(matches(k)[None], v[:, None, :], 0.0) for v in (rows, turned)]
                block = jnp.concatenate(pair, axis=1).reshape(128, 128)
                lhs[h, k, :, path * 128 : path * 128 + 128] = block.astype(bf16)
        return squares

    def tile_of(h, path, k, group):
        return xb[h, path, group * 8 : group * 8 + 8, k].reshape(128, 128)

    def cross(halves, group, first):
        squares = jnp.zeros((128, 128), f32) if first else sq_buf[group]
        for k in range(8):
            tiles = [tile_of(h, path, k, group) for h in halves for path in (0, 1)]
            for t in tiles:
                wide = t.astype(f32)
                squares = squares + wide * wide
            left = jnp.concatenate([lhs[h, k] for h in halves], axis=1)
            part = nt(left, jnp.concatenate(tiles, axis=1))
            s_buf[group, k] = part if first else s_buf[group, k] + part
        sq_buf[group] = squares

    pass_on(0, 1, None)
    pass_on(0, 2, None)
    pl.when(z >= 2)(answer_far)
    for plane in (0, 1, 2):
        relay(0, plane, None)

    @pl.when(z < 2)
    def _():
        pl.semaphore_wait(wrap_sem, 2 - z)
        z_copy(0, 2).start()
        pl.when(z == 0)(lambda: z_copy(0, 1).start())
        answer_far()

    o_copy(0, 1 - c).wait_recv()
    own_squares = build_lhs(0)
    for part in (0, 1):
        far_copy(part).wait_recv()
        spread(1, part)
    o_copy(1, c).start()
    for k in range(8):
        o_buf[1, c, k] = g_buf[1, 0, 0, k]
    for part in (0, 1):
        pass_on(1, 1, part)
        pass_on(1, 2, part)
        if part == 0:
            relay(1, 0, 0)
    relay(1, 0, 1)
    for part in (0, 1):
        for plane in (1, 2):
            relay(1, plane, part)
    o_copy(1, 1 - c).wait_recv()
    own_squares = own_squares + build_lhs(1)
    own_gain = concentration * lax.rsqrt(jnp.sum(own_squares, axis=1, keepdims=True) + epsilon)

    early = z_lo < 6
    for group in (0, 1):
        wait_slots(0, group)

    @pl.when(early)
    def _():
        for group in (0, 1):
            cross((0,), group, True)

    ones = jnp.ones((8, 384), bf16)
    lane = iota((128, 256), 1)
    own_lane = z_hi * 8 - 1000 * (1 - c)

    last = remote(fb.at[pl.ds(0, 4)], rb, ss_f, rs_f, partner)

    def filter_group(group):
        norm_squares = nt(ones, jnp.concatenate(pieces(sq_buf[group]), axis=1))
        gain = lax.rsqrt(norm_squares + epsilon) * own_gain
        for side in (0, 1):
            filter_side(group, gain, side)

    def filter_side(group, gain, side):
        for i in (4 * side, 4 * side + 2):
            two = [
                jnp.concatenate([s_buf[group, k, ii * 16 : ii * 16 + 16, :] for k in range(8)], axis=0)
                for ii in (i, i + 1)
            ]
            high, low = split(jnp.concatenate(two, axis=1))
            correlation = nn(forward, jnp.concatenate([high, low, high], axis=0))
            scale = jnp.concatenate([gain[i : i + 1], gain[i + 1 : i + 2]], axis=1)
            weights = jnp.exp(correlation * scale)
            if group == 0:
                same = lane - jnp.where(lane >= 128, 129, 0) == own_lane + i
                weights = jnp.where(same, 0.0, weights)
            high, low = split(weights)
            spectral = nn(backward, jnp.concatenate([high, low, high], axis=0))
            rounded = spectral.astype(bf16)
            for ii in (0, 1):
                part = spectral[:, ii * 128 : ii * 128 + 128]
                degree = jnp.broadcast_to(jnp.sum(part[0:1], axis=1, keepdims=True), (8, 128))
                fb[i + ii, 4] = degree if group == 0 else fb[i + ii, 4] + degree
                for k in range(8):
                    spec[k, (i + ii) * 16 : (i + ii) * 16 + 16, :] = rounded[
                        k * 16 : k * 16 + 16, ii * 128 : ii * 128 + 128
                    ]
        rows = pl.ds(side * 64, 64)
        totals = [None] * 4 if group == 0 else [acc[n, rows] for n in range(4)]
        for k in range(8):
            keep = jnp.concatenate([matches(k)] * 8, axis=0)
            tiles = [tile_of(h, path, k, group) for h in (0, 1) for path in (0, 1)]
            product = nn(spec[k, rows], jnp.concatenate(tiles, axis=1))
            for n in range(4):
                part = product[:, n * 128 : n * 128 + 128]
                if group == 0:
                    totals[n] = part if k == 0 else jnp.where(keep, part, totals[n])
                else:
                    totals[n] = totals[n] + jnp.where(keep, part, 0.0)
        for n in range(4):
            if group == 0:
                acc[n, rows] = totals[n]
            else:
                pair = totals[n].reshape(4, 16, 128)
                fb[4 * side : 4 * side + 4, n] = pair[:, :8] + rotate_parts(pair[:, 8:], -1.0)
        if group == 1 and side == 0:
            last.start()

    for group in (0, 1):
        wait_slots(1, group)

        @pl.when(early)
        def _():
            cross((1,), group, False)

        @pl.when(jnp.logical_not(early))
        def _():
            cross((0, 1), group, True)

        filter_group(group)

    last.wait()
    out_ref[...] = fb[4:8] + rb[...]

    for part in (0, 1):
        far_copy(part).wait_send()
    for h in (0, 1):
        parts = (0, 1) if h else (None,)
        for part in parts:
            z_copy(h, 1, part).wait_send()
            z_copy(h, 2, part).wait_send()
        o_copy(h, c).wait_send()
        for plane in (0, 1, 2):
            for j in (1, 2, 3):
                for part in parts:
                    a_copy(h, plane, j, part).wait_send()
        for core in (0, 1):
            for lot, count in enumerate((8, 4)):
                sent = xb.at[0, 0, pl.ds(0, count)]
                remote(sent, sent, ss_x.at[h, core, lot], rs_x.at[h, 0], partner).wait_send()

        def sent_over(core):
            sent = xb.at[0, 0, pl.ds(0, 4)]
            remote(sent, sent, ss_x.at[h, core, 2], rs_x.at[h, 0], partner).wait_send()

        pl.when(c == 0)(functools.partial(sent_over, 1))
        pl.when(c == 1)(functools.partial(sent_over, 0))


def order_kernel(total_ref, out_ref, log_ref):
    z_hi = lax.axis_index("off") // 2
    degree = total_ref[:, 4:5]
    v = (total_ref[:, :4] / degree).reshape(16, 8, 128)
    for bit in (1, 2, 4):
        v = jnp.where(lane_bit(v.shape, bit), pltpu.roll(v, bit, 1), v)
    for bit in (1, 2, 4):
        group = lane_bit(v.shape, 16 * bit)
        row = iota(v.shape, 1) // bit % 2 == 1
        down = lane_roll(pltpu.roll(v, 8 - bit, 1), 16 * bit)
        up = lane_roll(pltpu.roll(v, bit, 1), -16 * bit)
        v = jnp.where(group == row, v, jnp.where(group, down, up))
    permute = permutation()
    flat = sum(nt(p, permute) for p in pieces(v.reshape(128, 128))).reshape(4, 4, 8, 128)
    for h in (0, 1):
        for path in (0, 1):
            start = pl.multiple_of(((z_hi + h) % 2 * 2 + path) * 8, 8)
            out_ref[:, pl.ds(start, 8), :] = flat[:, 2 * h + path]
    logs = jnp.log(degree)
    for i in range(4):
        log_ref[i] = logs[i, 0, 0, 0]


def body(coefficients):
    vmem = pl.BlockSpec(memory_space=pltpu.VMEM)
    dma = pltpu.SemaphoreType.DMA
    total = pl.pallas_call(
        body_kernel,
        out_shape=jax.ShapeDtypeStruct((4, 5, 8, 128), f32),
        in_specs=[pl.BlockSpec(memory_space=pltpu.MemorySpace.HBM)],
        out_specs=vmem,
        scratch_shapes=[
            pltpu.VMEM((16, 8, 128), bf16),
            pltpu.VMEM((128, 128), f32),
            pltpu.VMEM((2, 2, 8, 16, 128), bf16),
            pltpu.VMEM((2, 3, 4, 8, 16, 128), bf16),
            pltpu.VMEM((2, 2, 16, 8, 16, 128), bf16),
            pltpu.VMEM((2, 8, 128, 256), bf16),
            pltpu.VMEM((2, 8, 128, 128), f32),
            pltpu.VMEM((2, 128, 128), f32),
            pltpu.VMEM((8, 128, 128), bf16),
            pltpu.VMEM((4, 128, 128), f32),
            pltpu.VMEM((8, 5, 8, 128), f32),
            pltpu.VMEM((4, 5, 8, 128), f32),
            dma,
            dma((2, 3, 2)), dma((2, 3, 2)),
            dma((2,)), dma((2,)),
            dma((2,)), dma((2,)),
            pltpu.SemaphoreType.REGULAR,
            pltpu.SemaphoreType.REGULAR,
            dma((2, 3, 3, 2)), dma((2, 3, 3, 2)),
            dma((2, 2, 3)), dma((2, 2)),
            dma, dma,
        ],
        compiler_params=pltpu.CompilerParams(
            collective_id=0, has_side_effects=True, vmem_limit_bytes=32 << 20
        ),
        name="graph_filter",
    )(coefficients)
    return pl.pallas_call(
        order_kernel,
        out_shape=(
            jax.ShapeDtypeStruct((4, 32, 128), f32),
            jax.ShapeDtypeStruct((4,), f32),
        ),
        in_specs=[vmem],
        out_specs=(vmem, pl.BlockSpec(memory_space=pltpu.SMEM)),
        compiler_params=pltpu.CompilerParams(vmem_limit_bytes=8 << 20),
        name="order",
    )(total)


def solution(mesh):
    return jax.shard_map(
        body,
        mesh=mesh,
        in_specs=(P("blk", "off", None),),
        out_specs=(P(("blk", "off"), None, None), P(("blk", "off"))),
        check_vma=False,
    )
```

```python
import functools
import functools
import math

import jax
import jax.numpy as jnp
from jax import lax
from jax.experimental import pallas as pl
from jax.experimental.pallas import tpu as pltpu
from jax.sharding import PartitionSpec as P

MESH = pl.DeviceIdType.MESH
epsilon = 1e-06
concentration = 40.0
f32, bf16 = jnp.float32, jnp.bfloat16


def nt(a, b):
    return lax.dot_general(a, b, (((1,), (1,)), ((), ())), preferred_element_type=f32)


def nn(a, b):
    return jnp.dot(a, b, preferred_element_type=f32)


def split(a):
    high = a.astype(bf16)
    return high, (a - high.astype(f32)).astype(bf16)


def iota(shape, dim):
    return lax.broadcasted_iota(jnp.int32, shape, dim)


def lane_bit(shape, bit):
    return iota(shape, len(shape) - 1) // bit % 2 == 1


def lane_roll(a, by):
    return pltpu.roll(a, by % 128, a.ndim - 1)


def permutation():
    place = iota((128, 128), 1)
    source = place // 8 % 2 * 64 + place // 16 * 8 + place % 8
    return jnp.where(iota((128, 128), 0) == source, 1.0, 0.0).astype(bf16)


def pieces(a):
    high, low = split(a)
    return [high, low, (a - high.astype(f32) - low.astype(f32)).astype(bf16)]


def rotate_parts(a, sign):
    imag = lane_bit(a.shape, 8)
    return jnp.where(imag, -sign * lane_roll(a, 8), sign * lane_roll(a, -8))


places = [
    (0, 0), (0, 1), (1, 0), (0, 3), (3, 0), (0, 2), (2, 0), (1, 1),
    (1, 3), (3, 1), (3, 3), (1, 2), (2, 1), (3, 2), (2, 3), (2, 2),
]
slot_of = {place: n for n, place in enumerate(places)}


def body_kernel(
    x_ref, out_ref,
    x_buf, yf, o_buf, g_buf, xb, lhs, s_buf, sq_buf, spec, acc, fb, rb,
    x_sem, ss_z, rs_z, ss_o, rs_o, ss_far, rs_far, ok_sem, wrap_sem, next_sem, ss_a, rs_a, ss_x, rs_x, ss_f, rs_f,
):
    b, o = lax.axis_index("blk"), lax.axis_index("off")
    x, y, z_lo = b % 4, b // 4 % 4, b // 16
    z_hi, c = o // 2, o % 2
    z = z_hi * 8 + z_lo

    load = pltpu.make_async_copy(x_ref, x_buf, x_sem)
    load.start()

    def device(dx, dy, dz, core):
        zz = (z + dz) % 16
        return (zz % 8 * 16 + (y + dy) % 4 * 4 + (x + dx) % 4, zz // 8 * 2 + core)

    def remote(src, dst, send, recv, to):
        return pltpu.make_async_remote_copy(
            src_ref=src, dst_ref=dst, send_sem=send, recv_sem=recv,
            device_id=to, device_id_type=MESH,
        )

    partner = device(0, 0, 0, 1 - c)
    opposite = device(0, 0, 8, c)
    barrier = pltpu.get_barrier_semaphore()
    peers = [partner]
    for d in (1, 3):
        for core in (0, 1):
            peers += [device(d, 0, 0, core), device(0, d, 0, core)]

    def announce(peer):
        pl.semaphore_signal(barrier, inc=1, device_id=peer, device_id_type=MESH)

    @pl.when(z_hi == 0)
    def _():
        announce(opposite)

    for peer in peers:
        announce(peer)

    late = (z + 2) // 16 + (z + 1) // 16
    first = (z + 15) // 16 + (z + 14) // 16
    for d in (1, 2):
        crossing = (z + d) // 16 == 1
        pl.when(jnp.logical_not(crossing))(lambda d=d: announce(device(0, 0, d, c)))
        pl.when(z - d < 0)(lambda d=d: announce(device(0, 0, -d, c)))

    permute = permutation()
    load.wait()
    yf[...] = nn(x_buf[...].astype(f32).reshape(128, 128).astype(bf16), permute)
    rows = [yf[pl.ds(r, 16, stride=8), :] for r in range(8)]
    for bit in (1, 2, 4):
        upper = lane_bit((16, 128), 16 * bit)
        for r in range(8):
            if r & bit == 0:
                low, high = rows[r], rows[r | bit]
                rows[r] = jnp.where(upper, lane_roll(high, 16 * bit), low)
                rows[r | bit] = jnp.where(upper, high, lane_roll(low, -16 * bit))
    for k in range(8):
        tile = rows[k].astype(bf16)
        g_buf[0, 0, 0, k] = tile
        o_buf[0, c, k] = tile

    pl.semaphore_wait(barrier, len(peers) + z_hi + late + first)
    for d in (1, 2):
        @pl.when((z + d) // 16 == 1)
        def _():
            pl.semaphore_signal(
                wrap_sem, inc=1, device_id=device(0, 0, d, c), device_id_type=MESH
            )

    own = g_buf.at[0, 0, 0]
    far_own = g_buf.at[1, 0, 0]

    def cut(ref, part):
        return ref if part is None else ref.at[pl.ds(4 * part, 4)]

    def far_copy(part):
        return remote(cut(own, part), cut(far_own, part), ss_far.at[part], rs_far.at[part], opposite)

    @pl.when(z_hi == 1)
    def _():
        far_copy(0).start()
        far_copy(1).start()
        pl.semaphore_signal(ok_sem, inc=1, device_id=opposite, device_id_type=MESH)

    for dx, dy in ((-1, 0), (0, -1)):
        pl.semaphore_signal(
            next_sem, inc=1, device_id=device(dx, dy, 0, c), device_id_type=MESH
        )

    def z_copy(h, plane, part=None):
        n = part or 0
        return remote(
            cut(g_buf.at[h, 0, 0], part), cut(g_buf.at[h, plane, 0], part),
            ss_z.at[h, plane, n], rs_z.at[h, plane, n], device(0, 0, -plane, c),
        )

    def o_copy(h, path):
        return remote(g_buf.at[h, 0, 0], o_buf.at[h, path], ss_o.at[h], rs_o.at[h], partner)

    def half_of(h, plane):
        return (h + (z_lo + plane) // 8) % 2

    def a_copy(h, plane, j, part):
        n = part or 0
        return remote(
            cut(g_buf.at[h, plane, 0], part), cut(g_buf.at[h, plane, j], part),
            ss_a.at[h, plane, j - 1, n], rs_a.at[h, plane, j - 1, n], device(-j * (1 - c), -j * c, 0, c),
        )

    def send_along(h, plane, part):
        for j in (1, 3, 2):
            if (h, plane, j) == (0, 0, 2):
                pl.semaphore_wait(next_sem, 2)
            a_copy(h, plane, j, part).start()

    def plane_of(j, d):
        first = (4 * ((y + d) % 4) + x) - (4 * y + (x + j) % 4)
        second = (4 * y + (x + d) % 4) - (4 * ((y + j) % 4) + x)
        return (first * (1 - c) + second * c + 15) // 16 * 2

    def slot(j, d):
        return slot_of[j, -d % 4] * (1 - c) + slot_of[-d % 4, j] * c

    def x_copy(h, plane, j, d, core, part):
        n = slot(j, d)
        lot = 2 if d == 0 else d // 3
        return remote(
            cut(g_buf.at[h, plane, j], part), cut(xb.at[half_of(h, plane), c, n], part),
            ss_x.at[h, core, lot], rs_x.at[h, n // 8], device(d * c, d * (1 - c), 0, core),
        )

    def keep_copy(h, plane, j, part):
        n = slot(j, 0)
        return pltpu.make_async_copy(
            cut(g_buf.at[h, plane, j], part), cut(xb.at[half_of(h, plane), c, n], part), rs_x.at[h, n // 8]
        )

    def send_across(h, plane, j, part):
        core = 0 if plane == 1 else 1

        def when(d, *more):
            wanted = [] if plane == 1 else [plane_of(j, d) == plane]
            tests = wanted + list(more)
            if not tests:
                return lambda f: f()
            return pl.when(functools.reduce(jnp.logical_and, tests))

        for d in (2, 1, 3):
            when(d)(lambda d=d: x_copy(h, plane, j, d, core, part).start())
        when(0, c != core)(lambda: x_copy(h, plane, j, 0, core, part).start())
        when(0, c == core)(lambda: keep_copy(h, plane, j, part).start())

    def wait_slots(h, group):
        region = xb.at[0, :, pl.ds(group * 8, 8)]
        pltpu.make_async_copy(region, region, rs_x.at[h, group]).wait()

    def answer_far():
        @pl.when(z_hi == 0)
        def _():
            pl.semaphore_wait(ok_sem, 1)
            far_copy(0).start()
            far_copy(1).start()

    def spread(h, part):
        if h == 0:
            pl.when(z >= 1)(lambda: z_copy(0, 1).start())
            pl.when(z >= 2)(lambda: z_copy(0, 2).start())
        else:
            z_copy(h, 1, part).start()
            z_copy(h, 2, part).start()
        send_along(h, 0, part)
        send_across(h, 0, 0, part)

    def pass_on(h, plane, part):
        z_copy(h, plane, part).wait_recv()
        send_along(h, plane, part)
        send_across(h, plane, 0, part)

    def relay(h, plane, part):
        for j in (1, 3, 2):
            a_copy(h, plane, j, part).wait_recv()
            send_across(h, plane, j, part)

    o_copy(0, c).start()
    spread(0, None)

    def frequency_of(q):
        k, u = q // 16, q % 8
        return 8 * k + (k - u + 8) % 8, q // 8 % 2

    def table(q_dim):
        q, s = iota((128, 128), q_dim), iota((128, 128), 1 - q_dim)
        m, part = frequency_of(q)
        phase = (m * s % 128).astype(f32) * (2.0 * math.pi / 128)
        return jnp.where(part == 0, jnp.cos(phase), -jnp.sin(phase))

    f_high, f_low = split(table(1))
    forward = jnp.concatenate([f_high, f_high, f_low], axis=1)
    b_high, b_low = split(table(0))
    backward = jnp.concatenate([b_high, b_high, b_low], axis=1)

    def matches(k):
        u, t = iota((8, 128), 0), iota((8, 128), 1) % 8
        return (u + t) % 8 == k

    def build_lhs(h):
        squares = jnp.zeros((8, 128), f32)
        for path in (0, 1):
            for k in range(8):
                both = o_buf[h, path, k].astype(f32)
                rows = jnp.where(z_hi == 0, both[:8], both[8:])
                rows = jnp.where(c == 0, pltpu.roll(rows, 4, 0), rows)
                squares = squares + rows * rows
                turned = rotate_parts(rows, 1.0)
                pair = [jnp.where(matches(k)[None], v[:, None, :], 0.0) for v in (rows, turned)]
                block = jnp.concatenate(pair, axis=1).reshape(128, 128)
                lhs[h, k, :, path * 128 : path * 128 + 128] = block.astype(bf16)
        return squares

    def tile_of(h, path, k, group):
        return xb[h, path, group * 8 : group * 8 + 8, k].reshape(128, 128)

    def cross(halves, group, first):
        squares = jnp.zeros((128, 128), f32) if first else sq_buf[group]
        for k in range(8):
            tiles = [tile_of(h, path, k, group) for h in halves for path in (0, 1)]
            for t in tiles:
                wide = t.astype(f32)
                squares = squares + wide * wide
            left = jnp.concatenate([lhs[h, k] for h in halves], axis=1)
            part = nt(left, jnp.concatenate(tiles, axis=1))
            s_buf[group, k] = part if first else s_buf[group, k] + part
        sq_buf[group] = squares

    pass_on(0, 1, None)
    pass_on(0, 2, None)
    pl.when(z >= 2)(answer_far)
    for plane in (0, 1, 2):
        relay(0, plane, None)

    @pl.when(z < 2)
    def _():
        pl.semaphore_wait(wrap_sem, 2 - z)
        z_copy(0, 2).start()
        pl.when(z == 0)(lambda: z_copy(0, 1).start())
        answer_far()

    o_copy(0, 1 - c).wait_recv()
    own_squares = build_lhs(0)
    for part in (0, 1):
        far_copy(part).wait_recv()
        spread(1, part)
    o_copy(1, c).start()
    for k in range(8):
        o_buf[1, c, k] = g_buf[1, 0, 0, k]
    for part in (0, 1):
        pass_on(1, 1, part)
        pass_on(1, 2, part)
        if part == 0:
            relay(1, 0, 0)
    relay(1, 0, 1)
    for part in (0, 1):
        for plane in (1, 2):
            relay(1, plane, part)
    o_copy(1, 1 - c).wait_recv()
    own_squares = own_squares + build_lhs(1)
    own_gain = concentration * lax.rsqrt(jnp.sum(own_squares, axis=1, keepdims=True) + epsilon)

    early = z_lo < 6
    for group in (0, 1):
        wait_slots(0, group)

    @pl.when(early)
    def _():
        for group in (0, 1):
            cross((0,), group, True)

    ones = jnp.ones((8, 384), bf16)
    lane = iota((128, 256), 1)
    own_lane = z_hi * 8 - 1000 * (1 - c)

    last = remote(fb.at[pl.ds(0, 4)], rb, ss_f, rs_f, partner)

    def filter_group(group):
        norm_squares = nt(ones, jnp.concatenate(pieces(sq_buf[group]), axis=1))
        gain = lax.rsqrt(norm_squares + epsilon) * own_gain
        for side in (0, 1):
            filter_side(group, gain, side)

    def filter_side(group, gain, side):
        for i in (4 * side, 4 * side + 2):
            two = [
                jnp.concatenate([s_buf[group, k, ii * 16 : ii * 16 + 16, :] for k in range(8)], axis=0)
                for ii in (i, i + 1)
            ]
            high, low = split(jnp.concatenate(two, axis=1))
            correlation = nn(forward, jnp.concatenate([high, low, high], axis=0))
            scale = jnp.concatenate([gain[i : i + 1], gain[i + 1 : i + 2]], axis=1)
            weights = jnp.exp(correlation * scale)
            if group == 0:
                same = lane - jnp.where(lane >= 128, 129, 0) == own_lane + i
                weights = jnp.where(same, 0.0, weights)
            high, low = split(weights)
            spectral = nn(backward, jnp.concatenate([high, low, high], axis=0))
            rounded = spectral.astype(bf16)
            for ii in (0, 1):
                part = spectral[:, ii * 128 : ii * 128 + 128]
                degree = jnp.broadcast_to(jnp.sum(part[0:1], axis=1, keepdims=True), (8, 128))
                fb[i + ii, 4] = degree if group == 0 else fb[i + ii, 4] + degree
                for k in range(8):
                    spec[k, (i + ii) * 16 : (i + ii) * 16 + 16, :] = rounded[
                        k * 16 : k * 16 + 16, ii * 128 : ii * 128 + 128
                    ]
        rows = pl.ds(side * 64, 64)
        totals = [None] * 4 if group == 0 else [acc[n, rows] for n in range(4)]
        for k in range(8):
            keep = jnp.concatenate([matches(k)] * 8, axis=0)
            tiles = [tile_of(h, path, k, group) for h in (0, 1) for path in (0, 1)]
            product = nn(spec[k, rows], jnp.concatenate(tiles, axis=1))
            for n in range(4):
                part = product[:, n * 128 : n * 128 + 128]
                if group == 0:
                    totals[n] = part if k == 0 else jnp.where(keep, part, totals[n])
                else:
                    totals[n] = totals[n] + jnp.where(keep, part, 0.0)
        for n in range(4):
            if group == 0:
                acc[n, rows] = totals[n]
            else:
                pair = totals[n].reshape(4, 16, 128)
                fb[4 * side : 4 * side + 4, n] = pair[:, :8] + rotate_parts(pair[:, 8:], -1.0)
        if group == 1 and side == 0:
            last.start()

    for group in (0, 1):
        wait_slots(1, group)

        @pl.when(early)
        def _():
            cross((1,), group, False)

        @pl.when(jnp.logical_not(early))
        def _():
            cross((0, 1), group, True)

        filter_group(group)

    last.wait()
    out_ref[...] = fb[4:8] + rb[...]

    for part in (0, 1):
        far_copy(part).wait_send()
    for h in (0, 1):
        parts = (0, 1) if h else (None,)
        for part in parts:
            z_copy(h, 1, part).wait_send()
            z_copy(h, 2, part).wait_send()
        o_copy(h, c).wait_send()
        for plane in (0, 1, 2):
            for j in (1, 2, 3):
                for part in parts:
                    a_copy(h, plane, j, part).wait_send()
        for core in (0, 1):
            for lot, count in enumerate((8, 4)):
                sent = xb.at[0, 0, pl.ds(0, count)]
                remote(sent, sent, ss_x.at[h, core, lot], rs_x.at[h, 0], partner).wait_send()

        def sent_over(core):
            sent = xb.at[0, 0, pl.ds(0, 4)]
            remote(sent, sent, ss_x.at[h, core, 2], rs_x.at[h, 0], partner).wait_send()

        pl.when(c == 0)(functools.partial(sent_over, 1))
        pl.when(c == 1)(functools.partial(sent_over, 0))


def order_kernel(total_ref, out_ref, log_ref):
    z_hi = lax.axis_index("off") // 2
    degree = total_ref[:, 4:5]
    v = (total_ref[:, :4] / degree).reshape(16, 8, 128)
    for bit in (1, 2, 4):
        v = jnp.where(lane_bit(v.shape, bit), pltpu.roll(v, bit, 1), v)
    for bit in (1, 2, 4):
        group = lane_bit(v.shape, 16 * bit)
        row = iota(v.shape, 1) // bit % 2 == 1
        down = lane_roll(pltpu.roll(v, 8 - bit, 1), 16 * bit)
        up = lane_roll(pltpu.roll(v, bit, 1), -16 * bit)
        v = jnp.where(group == row, v, jnp.where(group, down, up))
    permute = permutation()
    flat = sum(nt(p, permute) for p in pieces(v.reshape(128, 128))).reshape(4, 4, 8, 128)
    for h in (0, 1):
        for path in (0, 1):
            start = pl.multiple_of(((z_hi + h) % 2 * 2 + path) * 8, 8)
            out_ref[:, pl.ds(start, 8), :] = flat[:, 2 * h + path]
    logs = jnp.log(degree)
    for i in range(4):
        log_ref[i] = logs[i, 0, 0, 0]


def body(coefficients):
    vmem = pl.BlockSpec(memory_space=pltpu.VMEM)
    dma = pltpu.SemaphoreType.DMA
    total = pl.pallas_call(
        body_kernel,
        out_shape=jax.ShapeDtypeStruct((4, 5, 8, 128), f32),
        in_specs=[pl.BlockSpec(memory_space=pltpu.MemorySpace.HBM)],
        out_specs=vmem,
        scratch_shapes=[
            pltpu.VMEM((16, 8, 128), bf16),
            pltpu.VMEM((128, 128), f32),
            pltpu.VMEM((2, 2, 8, 16, 128), bf16),
            pltpu.VMEM((2, 3, 4, 8, 16, 128), bf16),
            pltpu.VMEM((2, 2, 16, 8, 16, 128), bf16),
            pltpu.VMEM((2, 8, 128, 256), bf16),
            pltpu.VMEM((2, 8, 128, 128), f32),
            pltpu.VMEM((2, 128, 128), f32),
            pltpu.VMEM((8, 128, 128), bf16),
            pltpu.VMEM((4, 128, 128), f32),
            pltpu.VMEM((8, 5, 8, 128), f32),
            pltpu.VMEM((4, 5, 8, 128), f32),
            dma,
            dma((2, 3, 2)), dma((2, 3, 2)),
            dma((2,)), dma((2,)),
            dma((2,)), dma((2,)),
            pltpu.SemaphoreType.REGULAR,
            pltpu.SemaphoreType.REGULAR,
            pltpu.SemaphoreType.REGULAR,
            dma((2, 3, 3, 2)), dma((2, 3, 3, 2)),
            dma((2, 2, 3)), dma((2, 2)),
            dma, dma,
        ],
        compiler_params=pltpu.CompilerParams(
            collective_id=0, has_side_effects=True, vmem_limit_bytes=32 << 20
        ),
        name="graph_filter",
    )(coefficients)
    return pl.pallas_call(
        order_kernel,
        out_shape=(
            jax.ShapeDtypeStruct((4, 32, 128), f32),
            jax.ShapeDtypeStruct((4,), f32),
        ),
        in_specs=[vmem],
        out_specs=(vmem, pl.BlockSpec(memory_space=pltpu.SMEM)),
        compiler_params=pltpu.CompilerParams(vmem_limit_bytes=8 << 20),
        name="order",
    )(total)


def solution(mesh):
    return jax.shard_map(
        body,
        mesh=mesh,
        in_specs=(P("blk", "off", None),),
        out_specs=(P(("blk", "off"), None, None), P(("blk", "off"))),
        check_vma=False,
    )
```

```python
import functools
import functools
import math

import jax
import jax.numpy as jnp
from jax import lax
from jax.experimental import pallas as pl
from jax.experimental.pallas import tpu as pltpu
from jax.sharding import PartitionSpec as P

MESH = pl.DeviceIdType.MESH
epsilon = 1e-06
concentration = 40.0
f32, bf16 = jnp.float32, jnp.bfloat16


def nt(a, b):
    return lax.dot_general(a, b, (((1,), (1,)), ((), ())), preferred_element_type=f32)


def nn(a, b):
    return jnp.dot(a, b, preferred_element_type=f32)


def split(a):
    high = a.astype(bf16)
    return high, (a - high.astype(f32)).astype(bf16)


def iota(shape, dim):
    return lax.broadcasted_iota(jnp.int32, shape, dim)


def lane_bit(shape, bit):
    return iota(shape, len(shape) - 1) // bit % 2 == 1


def lane_roll(a, by):
    return pltpu.roll(a, by % 128, a.ndim - 1)


def permutation():
    place = iota((128, 128), 1)
    source = place // 8 % 2 * 64 + place // 16 * 8 + place % 8
    return jnp.where(iota((128, 128), 0) == source, 1.0, 0.0).astype(bf16)


def pieces(a):
    high, low = split(a)
    return [high, low, (a - high.astype(f32) - low.astype(f32)).astype(bf16)]


def rotate_parts(a, sign):
    imag = lane_bit(a.shape, 8)
    return jnp.where(imag, -sign * lane_roll(a, 8), sign * lane_roll(a, -8))


places = [
    (0, 0), (0, 1), (1, 0), (0, 3), (3, 0), (0, 2), (2, 0), (1, 1),
    (1, 3), (3, 1), (3, 3), (1, 2), (2, 1), (3, 2), (2, 3), (2, 2),
]
slot_of = {place: n for n, place in enumerate(places)}


def body_kernel(
    x_ref, out_ref,
    yf, o_buf, g_buf, xb, lhs, s_buf, sq_buf, spec, acc, fb, rb,
    ss_z, rs_z, ss_o, rs_o, ss_far, rs_far, ok_sem, wrap_sem, next_sem, ss_a, rs_a, ss_x, rs_x, ss_f, rs_f,
):
    b, o = lax.axis_index("blk"), lax.axis_index("off")
    x, y, z_lo = b % 4, b // 4 % 4, b // 16
    z_hi, c = o // 2, o % 2
    z = z_hi * 8 + z_lo

    def device(dx, dy, dz, core):
        zz = (z + dz) % 16
        return (zz % 8 * 16 + (y + dy) % 4 * 4 + (x + dx) % 4, zz // 8 * 2 + core)

    def remote(src, dst, send, recv, to):
        return pltpu.make_async_remote_copy(
            src_ref=src, dst_ref=dst, send_sem=send, recv_sem=recv,
            device_id=to, device_id_type=MESH,
        )

    partner = device(0, 0, 0, 1 - c)
    opposite = device(0, 0, 8, c)
    barrier = pltpu.get_barrier_semaphore()
    peers = [partner]
    for d in (1, 3):
        for core in (0, 1):
            peers += [device(d, 0, 0, core), device(0, d, 0, core)]

    def announce(peer):
        pl.semaphore_signal(barrier, inc=1, device_id=peer, device_id_type=MESH)

    @pl.when(z_hi == 0)
    def _():
        announce(opposite)

    for peer in peers:
        announce(peer)

    late = (z + 2) // 16 + (z + 1) // 16
    first = (z + 15) // 16 + (z + 14) // 16
    for d in (1, 2):
        crossing = (z + d) // 16 == 1
        pl.when(jnp.logical_not(crossing))(lambda d=d: announce(device(0, 0, d, c)))
        pl.when(z - d < 0)(lambda d=d: announce(device(0, 0, -d, c)))

    permute = permutation()
    yf[...] = nn(x_ref[...].astype(f32).reshape(128, 128).astype(bf16), permute)
    rows = [yf[pl.ds(r, 16, stride=8), :] for r in range(8)]
    for bit in (1, 2, 4):
        upper = lane_bit((16, 128), 16 * bit)
        for r in range(8):
            if r & bit == 0:
                low, high = rows[r], rows[r | bit]
                rows[r] = jnp.where(upper, lane_roll(high, 16 * bit), low)
                rows[r | bit] = jnp.where(upper, high, lane_roll(low, -16 * bit))
    for k in range(8):
        tile = rows[k].astype(bf16)
        g_buf[0, 0, 0, k] = tile
        o_buf[0, c, k] = tile

    pl.semaphore_wait(barrier, len(peers) + z_hi + late + first)
    for d in (1, 2):
        @pl.when((z + d) // 16 == 1)
        def _():
            pl.semaphore_signal(
                wrap_sem, inc=1, device_id=device(0, 0, d, c), device_id_type=MESH
            )

    own = g_buf.at[0, 0, 0]
    far_own = g_buf.at[1, 0, 0]

    def cut(ref, part):
        return ref if part is None else ref.at[pl.ds(4 * part, 4)]

    def far_copy(part):
        return remote(cut(own, part), cut(far_own, part), ss_far.at[part], rs_far.at[part], opposite)

    @pl.when(z_hi == 1)
    def _():
        far_copy(0).start()
        far_copy(1).start()
        pl.semaphore_signal(ok_sem, inc=1, device_id=opposite, device_id_type=MESH)

    for dx, dy in ((-1, 0), (0, -1)):
        pl.semaphore_signal(
            next_sem, inc=1, device_id=device(dx, dy, 0, c), device_id_type=MESH
        )

    def z_copy(h, plane, part=None):
        n = part or 0
        return remote(
            cut(g_buf.at[h, 0, 0], part), cut(g_buf.at[h, plane, 0], part),
            ss_z.at[h, plane, n], rs_z.at[h, plane, n], device(0, 0, -plane, c),
        )

    def o_copy(h, path):
        return remote(g_buf.at[h, 0, 0], o_buf.at[h, path], ss_o.at[h], rs_o.at[h], partner)

    def half_of(h, plane):
        return (h + (z_lo + plane) // 8) % 2

    def a_copy(h, plane, j, part):
        n = part or 0
        return remote(
            cut(g_buf.at[h, plane, 0], part), cut(g_buf.at[h, plane, j], part),
            ss_a.at[h, plane, j - 1, n], rs_a.at[h, plane, j - 1, n], device(-j * (1 - c), -j * c, 0, c),
        )

    def send_along(h, plane, part):
        for j in (1, 3, 2):
            if (h, plane, j) == (0, 0, 2):
                pl.semaphore_wait(next_sem, 2)
            a_copy(h, plane, j, part).start()

    def plane_of(j, d):
        first = (4 * ((y + d) % 4) + x) - (4 * y + (x + j) % 4)
        second = (4 * y + (x + d) % 4) - (4 * ((y + j) % 4) + x)
        return (first * (1 - c) + second * c + 15) // 16 * 2

    def slot(j, d):
        return slot_of[j, -d % 4] * (1 - c) + slot_of[-d % 4, j] * c

    def x_copy(h, plane, j, d, core, part):
        n = slot(j, d)
        lot = 2 if d == 0 else d // 3
        return remote(
            cut(g_buf.at[h, plane, j], part), cut(xb.at[half_of(h, plane), c, n], part),
            ss_x.at[h, core, lot], rs_x.at[h, n // 8], device(d * c, d * (1 - c), 0, core),
        )

    def keep_copy(h, plane, j, part):
        n = slot(j, 0)
        return pltpu.make_async_copy(
            cut(g_buf.at[h, plane, j], part), cut(xb.at[half_of(h, plane), c, n], part), rs_x.at[h, n // 8]
        )

    def send_across(h, plane, j, part):
        core = 0 if plane == 1 else 1

        def when(d, *more):
            wanted = [] if plane == 1 else [plane_of(j, d) == plane]
            tests = wanted + list(more)
            if not tests:
                return lambda f: f()
            return pl.when(functools.reduce(jnp.logical_and, tests))

        for d in (2, 1, 3):
            when(d)(lambda d=d: x_copy(h, plane, j, d, core, part).start())
        when(0, c != core)(lambda: x_copy(h, plane, j, 0, core, part).start())
        when(0, c == core)(lambda: keep_copy(h, plane, j, part).start())

    def wait_slots(h, group):
        region = xb.at[0, :, pl.ds(group * 8, 8)]
        pltpu.make_async_copy(region, region, rs_x.at[h, group]).wait()

    def answer_far():
        @pl.when(z_hi == 0)
        def _():
            pl.semaphore_wait(ok_sem, 1)
            far_copy(0).start()
            far_copy(1).start()

    def spread(h, part):
        if h == 0:
            pl.when(z >= 1)(lambda: z_copy(0, 1).start())
            pl.when(z >= 2)(lambda: z_copy(0, 2).start())
        else:
            z_copy(h, 1, part).start()
            z_copy(h, 2, part).start()
        send_along(h, 0, part)
        send_across(h, 0, 0, part)

    def pass_on(h, plane, part):
        z_copy(h, plane, part).wait_recv()
        send_along(h, plane, part)
        send_across(h, plane, 0, part)

    def relay(h, plane, part):
        for j in (1, 3, 2):
            a_copy(h, plane, j, part).wait_recv()
            send_across(h, plane, j, part)

    o_copy(0, c).start()
    spread(0, None)

    def frequency_of(q):
        k, u = q // 16, q % 8
        return 8 * k + (k - u + 8) % 8, q // 8 % 2

    def table(q_dim):
        q, s = iota((128, 128), q_dim), iota((128, 128), 1 - q_dim)
        m, part = frequency_of(q)
        phase = (m * s % 128).astype(f32) * (2.0 * math.pi / 128)
        return jnp.where(part == 0, jnp.cos(phase), -jnp.sin(phase))

    f_high, f_low = split(table(1))
    forward = jnp.concatenate([f_high, f_high, f_low], axis=1)
    b_high, b_low = split(table(0))
    backward = jnp.concatenate([b_high, b_high, b_low], axis=1)

    def matches(k):
        u, t = iota((8, 128), 0), iota((8, 128), 1) % 8
        return (u + t) % 8 == k

    def build_lhs(h):
        squares = jnp.zeros((8, 128), f32)
        for path in (0, 1):
            for k in range(8):
                both = o_buf[h, path, k].astype(f32)
                rows = jnp.where(z_hi == 0, both[:8], both[8:])
                rows = jnp.where(c == 0, pltpu.roll(rows, 4, 0), rows)
                squares = squares + rows * rows
                turned = rotate_parts(rows, 1.0)
                pair = [jnp.where(matches(k)[None], v[:, None, :], 0.0) for v in (rows, turned)]
                block = jnp.concatenate(pair, axis=1).reshape(128, 128)
                lhs[h, k, :, path * 128 : path * 128 + 128] = block.astype(bf16)
        return squares

    def tile_of(h, path, k, group):
        return xb[h, path, group * 8 : group * 8 + 8, k].reshape(128, 128)

    def cross(halves, group, first):
        squares = jnp.zeros((128, 128), f32) if first else sq_buf[group]
        for k in range(8):
            tiles = [tile_of(h, path, k, group) for h in halves for path in (0, 1)]
            for t in tiles:
                wide = t.astype(f32)
                squares = squares + wide * wide
            left = jnp.concatenate([lhs[h, k] for h in halves], axis=1)
            part = nt(left, jnp.concatenate(tiles, axis=1))
            s_buf[group, k] = part if first else s_buf[group, k] + part
        sq_buf[group] = squares

    pass_on(0, 1, None)
    pass_on(0, 2, None)
    pl.when(z >= 2)(answer_far)
    for plane in (1, 0, 2):
        relay(0, plane, None)

    @pl.when(z < 2)
    def _():
        pl.semaphore_wait(wrap_sem, 2 - z)
        z_copy(0, 2).start()
        pl.when(z == 0)(lambda: z_copy(0, 1).start())
        answer_far()

    o_copy(0, 1 - c).wait_recv()
    own_squares = build_lhs(0)
    for part in (0, 1):
        far_copy(part).wait_recv()
        spread(1, part)
    o_copy(1, c).start()
    for k in range(8):
        o_buf[1, c, k] = g_buf[1, 0, 0, k]
    pass_on(1, 1, 0)
    relay(1, 0, 0)
    pass_on(1, 2, 0)
    pass_on(1, 1, 1)
    relay(1, 0, 1)
    pass_on(1, 2, 1)
    for part in (0, 1):
        for plane in (1, 2):
            relay(1, plane, part)
    o_copy(1, 1 - c).wait_recv()
    own_squares = own_squares + build_lhs(1)
    own_gain = concentration * lax.rsqrt(jnp.sum(own_squares, axis=1, keepdims=True) + epsilon)

    early = z_lo < 6
    for group in (0, 1):
        wait_slots(0, group)

    @pl.when(early)
    def _():
        for group in (0, 1):
            cross((0,), group, True)

    ones = jnp.ones((8, 384), bf16)
    lane = iota((128, 256), 1)
    own_lane = z_hi * 8 - 1000 * (1 - c)

    last = remote(fb.at[pl.ds(0, 4)], rb, ss_f, rs_f, partner)

    def filter_group(group):
        norm_squares = nt(ones, jnp.concatenate(pieces(sq_buf[group]), axis=1))
        gain = lax.rsqrt(norm_squares + epsilon) * own_gain
        for side in (0, 1):
            filter_side(group, gain, side)

    def filter_side(group, gain, side):
        for i in (4 * side, 4 * side + 2):
            two = [
                jnp.concatenate([s_buf[group, k, ii * 16 : ii * 16 + 16, :] for k in range(8)], axis=0)
                for ii in (i, i + 1)
            ]
            high, low = split(jnp.concatenate(two, axis=1))
            correlation = nn(forward, jnp.concatenate([high, low, high], axis=0))
            scale = jnp.concatenate([gain[i : i + 1], gain[i + 1 : i + 2]], axis=1)
            weights = jnp.exp(correlation * scale)
            if group == 0:
                same = lane - jnp.where(lane >= 128, 129, 0) == own_lane + i
                weights = jnp.where(same, 0.0, weights)
            high, low = split(weights)
            spectral = nn(backward, jnp.concatenate([high, low, high], axis=0))
            rounded = spectral.astype(bf16)
            for ii in (0, 1):
                part = spectral[:, ii * 128 : ii * 128 + 128]
                degree = jnp.broadcast_to(jnp.sum(part[0:1], axis=1, keepdims=True), (8, 128))
                fb[i + ii, 4] = degree if group == 0 else fb[i + ii, 4] + degree
                for k in range(8):
                    spec[k, (i + ii) * 16 : (i + ii) * 16 + 16, :] = rounded[
                        k * 16 : k * 16 + 16, ii * 128 : ii * 128 + 128
                    ]
        rows = pl.ds(side * 64, 64)
        totals = [None] * 4 if group == 0 else [acc[n, rows] for n in range(4)]
        for k in range(8):
            keep = jnp.concatenate([matches(k)] * 8, axis=0)
            tiles = [tile_of(h, path, k, group) for h in (0, 1) for path in (0, 1)]
            product = nn(spec[k, rows], jnp.concatenate(tiles, axis=1))
            for n in range(4):
                part = product[:, n * 128 : n * 128 + 128]
                if group == 0:
                    totals[n] = part if k == 0 else jnp.where(keep, part, totals[n])
                else:
                    totals[n] = totals[n] + jnp.where(keep, part, 0.0)
        for n in range(4):
            if group == 0:
                acc[n, rows] = totals[n]
            else:
                pair = totals[n].reshape(4, 16, 128)
                fb[4 * side : 4 * side + 4, n] = pair[:, :8] + rotate_parts(pair[:, 8:], -1.0)
        if group == 1 and side == 0:
            last.start()

    for group in (0, 1):
        wait_slots(1, group)

        @pl.when(early)
        def _():
            cross((1,), group, False)

        @pl.when(jnp.logical_not(early))
        def _():
            cross((0, 1), group, True)

        filter_group(group)

    last.wait()
    out_ref[...] = fb[4:8] + rb[...]

    for part in (0, 1):
        far_copy(part).wait_send()
    for h in (0, 1):
        parts = (0, 1) if h else (None,)
        for part in parts:
            z_copy(h, 1, part).wait_send()
            z_copy(h, 2, part).wait_send()
        o_copy(h, c).wait_send()
        for plane in (0, 1, 2):
            for j in (1, 2, 3):
                for part in parts:
                    a_copy(h, plane, j, part).wait_send()
        for core in (0, 1):
            for lot, count in enumerate((8, 4)):
                sent = xb.at[0, 0, pl.ds(0, count)]
                remote(sent, sent, ss_x.at[h, core, lot], rs_x.at[h, 0], partner).wait_send()

        def sent_over(core):
            sent = xb.at[0, 0, pl.ds(0, 4)]
            remote(sent, sent, ss_x.at[h, core, 2], rs_x.at[h, 0], partner).wait_send()

        pl.when(c == 0)(functools.partial(sent_over, 1))
        pl.when(c == 1)(functools.partial(sent_over, 0))


def order_kernel(total_ref, out_ref, log_ref):
    z_hi = lax.axis_index("off") // 2
    degree = total_ref[:, 4:5]
    v = (total_ref[:, :4] / degree).reshape(16, 8, 128)
    for bit in (1, 2, 4):
        v = jnp.where(lane_bit(v.shape, bit), pltpu.roll(v, bit, 1), v)
    for bit in (1, 2, 4):
        group = lane_bit(v.shape, 16 * bit)
        row = iota(v.shape, 1) // bit % 2 == 1
        down = lane_roll(pltpu.roll(v, 8 - bit, 1), 16 * bit)
        up = lane_roll(pltpu.roll(v, bit, 1), -16 * bit)
        v = jnp.where(group == row, v, jnp.where(group, down, up))
    permute = permutation()
    flat = sum(nt(p, permute) for p in pieces(v.reshape(128, 128))).reshape(4, 4, 8, 128)
    for h in (0, 1):
        for path in (0, 1):
            start = pl.multiple_of(((z_hi + h) % 2 * 2 + path) * 8, 8)
            out_ref[:, pl.ds(start, 8), :] = flat[:, 2 * h + path]
    logs = jnp.log(degree)
    for i in range(4):
        log_ref[i] = logs[i, 0, 0, 0]


def body(coefficients):
    vmem = pl.BlockSpec(memory_space=pltpu.VMEM)
    dma = pltpu.SemaphoreType.DMA
    total = pl.pallas_call(
        body_kernel,
        out_shape=jax.ShapeDtypeStruct((4, 5, 8, 128), f32),
        in_specs=[vmem],
        out_specs=vmem,
        scratch_shapes=[
            pltpu.VMEM((128, 128), f32),
            pltpu.VMEM((2, 2, 8, 16, 128), bf16),
            pltpu.VMEM((2, 3, 4, 8, 16, 128), bf16),
            pltpu.VMEM((2, 2, 16, 8, 16, 128), bf16),
            pltpu.VMEM((2, 8, 128, 256), bf16),
            pltpu.VMEM((2, 8, 128, 128), f32),
            pltpu.VMEM((2, 128, 128), f32),
            pltpu.VMEM((8, 128, 128), bf16),
            pltpu.VMEM((4, 128, 128), f32),
            pltpu.VMEM((8, 5, 8, 128), f32),
            pltpu.VMEM((4, 5, 8, 128), f32),
            dma((2, 3, 2)), dma((2, 3, 2)),
            dma((2,)), dma((2,)),
            dma((2,)), dma((2,)),
            pltpu.SemaphoreType.REGULAR,
            pltpu.SemaphoreType.REGULAR,
            pltpu.SemaphoreType.REGULAR,
            dma((2, 3, 3, 2)), dma((2, 3, 3, 2)),
            dma((2, 2, 3)), dma((2, 2)),
            dma, dma,
        ],
        compiler_params=pltpu.CompilerParams(
            collective_id=0, has_side_effects=True, vmem_limit_bytes=32 << 20
        ),
        name="graph_filter",
    )(coefficients)
    return pl.pallas_call(
        order_kernel,
        out_shape=(
            jax.ShapeDtypeStruct((4, 32, 128), f32),
            jax.ShapeDtypeStruct((4,), f32),
        ),
        in_specs=[vmem],
        out_specs=(vmem, pl.BlockSpec(memory_space=pltpu.SMEM)),
        compiler_params=pltpu.CompilerParams(vmem_limit_bytes=8 << 20),
        name="order",
    )(total)


def solution(mesh):
    return jax.shard_map(
        body,
        mesh=mesh,
        in_specs=(P("blk", "off", None),),
        out_specs=(P(("blk", "off"), None, None), P(("blk", "off"))),
        check_vma=False,
    )
```
